32 devices in a mesh: scan: 8 (over z, y), beam: 4 (over x, core).
Axes of the slice: x: 2, y: 2, z: 4, core: 2. Of those that a mesh axis runs over, the one named last changes fastest.
Arguments:
- smatrix: bfloat16 [2, 1024, 512, 128], P(None, 'beam', 'scan'), may hold values from -6 to 6
- beam_freq: int32 [2, 1024], P(None, 'beam'), may hold values from -32 to 31
- beam_amp: float32 [2, 1024], P(None, 'beam'), may hold values from -0.1875 to 0.1875
- row_offset: int32 [512], P('scan'), may hold values from 0 to 63
- col_offset: int32 [512], P('scan'), may hold values from 0 to 127
- counts: int32 [8], P('scan'), may hold values from 16 to 64, as said below
- amplitude: float32 [512, 128, 128], P('scan'), may hold values from 0.25 to 2
Outputs:
- grad_smatrix: bfloat16 [2, 1024, 512, 128], P(None, 'beam', 'scan')
The draws below stay inside these ranges and needn't reach their ends.
Inputs may be any that keep to these rules, and one draw needn't show every extreme that they name: `counts`: slots of a tile at or past its count are unused; some tile holds exactly 64 live positions.
All inputs are finite; a program needn't handle non-finite values.
Results may differ from the reference program's by a relative error of at most 0.0063.
Values may be sent and summed in bfloat16 or wider, within the bound.
A program may use at most 192 MiB of HBM per device.

```python
import math
import jax
import jax.numpy as jnp
from jax import lax

WIN = 128
BEAMS = 1024
POS_DEV = 64
TY = 64
NY = 512
POSITIONS = 512
N_SCAN = 8


def draw_counts(key, part):
    first_key = jax.random.fold_in(key, 11)
    second_key = jax.random.fold_in(key, 12)
    values = jax.random.randint(first_key, (N_SCAN,), max(1, POS_DEV // 4), POS_DEV + 1)
    chosen = jax.random.randint(second_key, (), 0, N_SCAN)
    return jnp.where(jnp.arange(N_SCAN) == chosen, POS_DEV, values).astype(jnp.int32)


def set_ends(values, own_key, low, largest):
    longest = values.shape.index(max(values.shape))
    spots = []
    for shift in (0, 1):
        where = [jax.random.randint(jax.random.fold_in(own_key, axis), (), 0, length) for axis, length in enumerate(values.shape)]
        where[longest] = (where[longest] + shift) % values.shape[longest]
        spots.append(tuple(where))
    return values.at[spots[0]].set(low).at[spots[1]].set(largest)


def steps_of(stream_key, dims, pieces, smallest, high):
    def one(dim, parts):
        draws = jax.random.uniform(jax.random.fold_in(jax.random.fold_in(stream_key, 6), dim), (parts,), jnp.float32, smallest / len(pieces), high / len(pieces))
        return jnp.repeat(jnp.exp(draws), dims[dim] // parts).reshape((-1,) + (1,) * (len(dims) - dim - 1))

    loudness = one(*pieces[0])
    for cut in pieces[1:]:
        loudness = loudness * one(*cut)
    return loudness


def scatter_about(rng, dims, width, most, cuts=(), kind=jnp.bfloat16):
    result = width * jax.random.normal(rng, dims, jnp.float32)
    if cuts:
        result = result * steps_of(rng, dims, cuts, -0.22, 0.18)
    return jnp.clip(result, -most, most).astype(kind)


def setup_inputs(seed: int = 0) -> dict:
    key_list = jax.random.split(jax.random.key(seed), 8)
    return {
        "smatrix": scatter_about(key_list[0], (2, BEAMS, NY, WIN), 1.0, 6.0, ((1, 4), (2, 8))),
        "beam_freq": set_ends(jax.random.randint(key_list[1], (2, BEAMS), 0 - WIN // 4, WIN // 4), jax.random.fold_in(key_list[1], 1), 0 - WIN // 4, (WIN // 4) - 1).astype(jnp.int32),
        "beam_amp": scatter_about(key_list[2], (2, BEAMS), BEAMS ** -0.5, 0.1875, ((1, 4),), jnp.float32),
        "row_offset": set_ends(jax.random.randint(key_list[3], (POSITIONS,), 0, TY), jax.random.fold_in(key_list[3], 1), 0, TY - 1).astype(jnp.int32),
        "col_offset": set_ends(jax.random.randint(key_list[4], (POSITIONS,), 0, WIN), jax.random.fold_in(key_list[4], 1), 0, WIN - 1).astype(jnp.int32),
        "counts": draw_counts(jax.random.fold_in(key_list[7], 71), 0),
        "amplitude": jnp.clip(0.25 + 1.75 * jax.random.uniform(key_list[6], (POSITIONS, WIN, WIN), jnp.float32) ** steps_of(key_list[6], (POSITIONS, WIN, WIN), ((0, 8),), -0.2, 0.2), 0.25, 2.0),
    }


TWO_PI = 6.283185307179586
ETA = 0.1

def coefficients(tile_rows, tile_cols, tile_ids, beam_freq, beam_amp, strip_rows, field_rows, window):
    global_rows = tile_ids * strip_rows + tile_rows
    along_rows = beam_freq[0][None, :] * global_rows[:, None] % field_rows
    along_cols = beam_freq[1][None, :] * tile_cols[:, None] % window
    phase_turns = along_rows.astype(jnp.float32) / field_rows + along_cols.astype(jnp.float32) / window
    phase_angle = -TWO_PI * phase_turns
    cos_part = jnp.cos(phase_angle)
    sin_part = jnp.sin(phase_angle)
    coef_re = beam_amp[0][None, :] * cos_part - beam_amp[1][None, :] * sin_part
    coef_im = beam_amp[0][None, :] * sin_part + beam_amp[1][None, :] * cos_part
    return (coef_re.astype(jnp.bfloat16), coef_im.astype(jnp.bfloat16))

def forward_matrix(coef_re, coef_im):
    real_rows = jnp.concatenate([coef_re, -coef_im], axis=1)
    imag_rows = jnp.concatenate([coef_im, coef_re], axis=1)
    return jnp.concatenate([real_rows, imag_rows], axis=0)

def backward_matrix(coef_re, coef_im):
    real_rows = jnp.concatenate([coef_re.T, coef_im.T], axis=1)
    imag_rows = jnp.concatenate([-coef_im.T, coef_re.T], axis=1)
    return jnp.concatenate([real_rows, imag_rows], axis=0)

def dft_tables(window):
    counter = jnp.arange(window, dtype=jnp.int32)
    product = counter[:, None] * counter[None, :] % window
    turn_angle = product.astype(jnp.float32) * (TWO_PI / window)
    norm_scale = 1.0 / math.sqrt(window)
    return (jnp.cos(turn_angle) * norm_scale, -jnp.sin(turn_angle) * norm_scale)

def transform(real_in, imag_in, table_re, table_im):
    highest = lax.Precision.HIGHEST
    left_re = jnp.einsum('jk,qkl->qjl', table_re, real_in, precision=highest) - jnp.einsum('jk,qkl->qjl', table_im, imag_in, precision=highest)
    left_im = jnp.einsum('jk,qkl->qjl', table_re, imag_in, precision=highest) + jnp.einsum('jk,qkl->qjl', table_im, real_in, precision=highest)
    out_re = jnp.einsum('qjk,kl->qjl', left_re, table_re, precision=highest) - jnp.einsum('qjk,kl->qjl', left_im, table_im, precision=highest)
    out_im = jnp.einsum('qjk,kl->qjl', left_re, table_im, precision=highest) + jnp.einsum('qjk,kl->qjl', left_im, table_re, precision=highest)
    return (out_re, out_im)

def far_field_gradient(wave_re, wave_im, measured, live_rows, tables):
    table_re, table_im = tables
    far_re, far_im = transform(wave_re, wave_im, table_re, table_im)
    modulus = jnp.sqrt(far_re * far_re + far_im * far_im + ETA)
    keep_share = 1.0 - measured / modulus
    back_re, back_im = transform(far_re * keep_share, far_im * keep_share, table_re, -table_im)
    live_mask = live_rows[:, None, None]
    return jnp.stack([back_re * live_mask, back_im * live_mask], axis=0).astype(jnp.bfloat16)

def selection(tile_rows, window, total_rows):
    field_index = jnp.arange(total_rows, dtype=jnp.int32)
    window_index = jnp.arange(window, dtype=jnp.int32)
    target = tile_rows[:, None, None] + window_index[None, None, :]
    return (field_index[None, :, None] == target).astype(jnp.float32)

def take_window(strip_waves, tile_rows, window):
    picker = selection(tile_rows, window, strip_waves.shape[2])
    return jnp.einsum('pyj,cpyx->cpjx', picker, strip_waves.astype(jnp.float32), precision=lax.Precision.HIGHEST)

def place_rows(wave_grads, tile_rows, total_rows):
    picker = selection(tile_rows, wave_grads.shape[2], total_rows)
    placed = jnp.einsum('pyj,cpjx->cpyx', picker, wave_grads.astype(jnp.float32))
    return placed.astype(jnp.bfloat16)

def reference(smatrix, beam_freq, beam_amp, row_offset, col_offset, counts, amplitude):
    tables = dft_tables(WIN)
    field_rows = TY * N_SCAN

    def tile_coefficients(tile_id):
        tile_rows = lax.dynamic_slice_in_dim(row_offset, tile_id * POS_DEV, POS_DEV)
        tile_cols = lax.dynamic_slice_in_dim(col_offset, tile_id * POS_DEV, POS_DEV)
        tile_ids = jnp.full((POS_DEV,), tile_id, jnp.int32)
        return (tile_rows, coefficients(tile_rows, tile_cols, tile_ids, beam_freq, beam_amp, TY, field_rows, WIN))

    def strip_of(strip_index):
        return lax.dynamic_slice_in_dim(smatrix, (strip_index % N_SCAN * TY).astype(jnp.int32), TY, axis=2)

    def forward_tile(tile_id):
        tile_rows, (coef_re, coef_im) = tile_coefficients(tile_id)
        extended = jnp.concatenate([strip_of(tile_id + distance) for distance in range(3)], axis=2).reshape(2 * BEAMS, 3 * TY * WIN)
        strip_waves = jnp.dot(forward_matrix(coef_re, coef_im), extended, preferred_element_type=jnp.float32).reshape(2, POS_DEV, 3 * TY, WIN)
        windows = take_window(strip_waves, tile_rows, WIN)
        live_rows = (jnp.arange(POS_DEV, dtype=jnp.int32) < lax.dynamic_index_in_dim(counts, tile_id, keepdims=False)).astype(jnp.float32)
        measured = lax.dynamic_slice_in_dim(amplitude, tile_id * POS_DEV, POS_DEV)
        return far_field_gradient(windows[0], windows[1], measured, live_rows, tables)
    tile_list = jnp.arange(N_SCAN, dtype=jnp.int32)
    all_grads = lax.map(forward_tile, tile_list)

    def strip_gradient(strip_id):
        grad_parts = []
        re_parts = []
        im_parts = []
        for distance in range(3):
            tile_id = ((strip_id - distance) % N_SCAN).astype(jnp.int32)
            tile_rows, (coef_re, coef_im) = tile_coefficients(tile_id)
            wave_grads = lax.dynamic_index_in_dim(all_grads, tile_id, keepdims=False)
            placed = place_rows(wave_grads, tile_rows, 3 * TY)
            grad_parts.append(placed[:, :, distance * TY:(distance + 1) * TY])
            re_parts.append(coef_re)
            im_parts.append(coef_im)
        gathered = jnp.stack(grad_parts, axis=1).reshape(6 * POS_DEV, TY * WIN)
        matrix = backward_matrix(jnp.concatenate(re_parts, axis=0), jnp.concatenate(im_parts, axis=0))
        return jnp.dot(matrix, gathered, preferred_element_type=jnp.float32).astype(jnp.bfloat16).reshape(2, BEAMS, TY, WIN)
    strips = lax.map(strip_gradient, tile_list)
    return jnp.transpose(strips, (1, 2, 0, 3, 4)).reshape(2, BEAMS, N_SCAN * TY, WIN)
```

```python
import functools
import math

import jax
import jax.numpy as jnp
from jax import lax
from jax.experimental import pallas as pl
from jax.experimental.pallas import tpu as pltpu
from jax.sharding import PartitionSpec as P

TWO_PI = 6.283185307179586
ETA = 0.1
F32 = jnp.float32
BF16 = jnp.bfloat16
LINK = jnp.float16
CORE_LINK = jnp.float32
CHUNKS = 2


def passed_along(value, axis, by):
    devices = lax.axis_size(axis)
    return lax.ppermute(value, axis, [(i, (i + by) % devices) for i in range(devices)])


def swapped(value, axis, bit):
    devices = lax.axis_size(axis)
    return lax.ppermute(value, axis, [(i, i ^ bit) for i in range(devices)])


def coefficients(
    global_rows, tile_cols, beam_freq, beam_amp, field_rows, window
):
    along_rows = beam_freq[0][None, :] * global_rows[:, None] % field_rows
    along_cols = beam_freq[1][None, :] * tile_cols[:, None] % window
    phase_turns = along_rows.astype(F32) / field_rows + along_cols.astype(F32) / window
    phase_angle = -TWO_PI * phase_turns
    cos_part = jnp.cos(phase_angle)
    sin_part = jnp.sin(phase_angle)
    coef_re = beam_amp[0][None, :] * cos_part - beam_amp[1][None, :] * sin_part
    coef_im = beam_amp[0][None, :] * sin_part + beam_amp[1][None, :] * cos_part
    return (coef_re.astype(BF16), coef_im.astype(BF16))


def dft_tables(window):
    counter = jnp.arange(window, dtype=jnp.int32)
    product = counter[:, None] * counter[None, :] % window
    turn_angle = product.astype(F32) * (TWO_PI / window)
    norm_scale = 1.0 / math.sqrt(window)
    return (jnp.cos(turn_angle) * norm_scale, -jnp.sin(turn_angle) * norm_scale)


def split_two(value):
    high = value.astype(BF16)
    return high, (value - high.astype(F32)).astype(BF16)


def forward_kernel(shares, kept, block_rows, offset, bounds_ref, matrix_ref, strip_ref, *refs):
    kept_ref, sent_ref, wide = refs
    depth = matrix_ref.shape[1]
    window = strip_ref.shape[3]
    group = matrix_ref.shape[0] // (3 * shares)
    wide[...] = strip_ref[...].reshape(depth * block_rows, window).astype(F32)
    first = (pl.program_id(0) + offset) * block_rows
    low = bounds_ref[0]
    high = bounds_ref[1]
    for row in range(0, block_rows, 2):
        rhs = jnp.concatenate(
            [wide[pl.ds(row + k, depth, stride=block_rows), :] for k in range(2)], axis=1
        ).astype(BF16)
        sums = jnp.dot(matrix_ref[...], rhs, preferred_element_type=F32)
        for k in range(2):
            here = first + row + k
            inside = (low <= here) & (here < high)
            part = jnp.where(inside, sums[:, k * window : (k + 1) * window], 0.0)
            for distance in range(3):
                for share in range(shares):
                    at = (distance * shares + share) * group
                    piece = part[at : at + group]
                    if share < kept:
                        kept_ref[share, distance, row + k] = piece
                    else:
                        sent_ref[share - kept, distance, row + k] = piece.astype(sent_ref.dtype)


def forward(matrix, bounds, strip, shares, chunk, chunk_rows, block_rows=16):
    _, beams, strip_rows, window = strip.shape
    kept = shares // 2
    group = matrix.shape[0] // (3 * shares)
    steps = chunk_rows // block_rows
    offset = chunk * steps
    shape = (kept, 3, chunk_rows, group, window)
    spec = pl.BlockSpec((kept, 3, block_rows, group, window), lambda i: (0, 0, i, 0, 0))
    return pl.pallas_call(
        functools.partial(forward_kernel, shares, kept, block_rows, offset),
        grid=(steps,),
        out_shape=[jax.ShapeDtypeStruct(shape, F32), jax.ShapeDtypeStruct(shape, CORE_LINK)],
        in_specs=[
            pl.BlockSpec(bounds.shape, lambda i: (0, 0, 0)),
            pl.BlockSpec(matrix.shape, lambda i: (0, 0)),
            pl.BlockSpec((2, beams, block_rows, window), lambda i: (0, 0, i + offset, 0)),
        ],
        out_specs=[spec, spec],
        scratch_shapes=[pltpu.VMEM((2 * beams * block_rows, window), F32)],
        compiler_params=pltpu.CompilerParams(vmem_limit_bytes=48 << 20),
        cost_estimate=pl.CostEstimate(
            flops=2 * matrix.size * chunk_rows * window,
            bytes_accessed=4 * beams * chunk_rows * window + 4 * matrix.shape[0] * chunk_rows * window,
            transcendentals=0,
        ),
    )(bounds, matrix, strip)


def backward_kernel(shares, block_rows, offset, bounds_ref, matrix_ref, *refs):
    parts, out_ref, wide = refs[: 2 * shares], refs[-2], refs[-1]
    depth = matrix_ref.shape[0]
    window = out_ref.shape[3]
    first = (pl.program_id(0) + offset) * block_rows
    low = bounds_ref[0]
    high = bounds_ref[1]
    for row in range(0, block_rows, 2):
        sides = []
        for k in range(2):
            here = first + row + k
            inside = (low <= here) & (here < high)
            pieces = [part[0, row + k] for part in parts[:shares]]
            for later in range(2):
                pieces += [part[later, row + k] for part in parts[shares:]]
            tall = jnp.concatenate(pieces, axis=0)
            sides.append(jnp.where(inside, tall.astype(F32), 0.0).astype(BF16))
        sums = jnp.dot(
            matrix_ref[...], jnp.concatenate(sides, axis=1), preferred_element_type=F32
        )
        for k in range(2):
            wide[pl.ds(row + k, depth, stride=block_rows), :] = sums[:, k * window : (k + 1) * window]
    out_ref[...] = wide[...].reshape(out_ref.shape).astype(BF16)


def backward(matrix, bounds, parts, shares, beams, strip_rows, chunk, before, block_rows=16):
    _, chunk_rows, group, window = parts[0].shape
    steps = chunk_rows // block_rows
    offset = chunk * steps
    operands = [bounds, matrix] + parts
    in_specs = [
        pl.BlockSpec(bounds.shape, lambda i: (0, 0, 0)),
        pl.BlockSpec(matrix.shape, lambda i: (0, 0)),
    ] + [pl.BlockSpec((p.shape[0], block_rows, group, window), lambda i: (0, i, 0, 0)) for p in parts]
    aliases = {}
    if before is not None:
        aliases = {len(operands): 0}
        operands.append(before)
        in_specs.append(pl.BlockSpec(memory_space=pl.ANY))
    return pl.pallas_call(
        functools.partial(backward_kernel, shares, block_rows, offset),
        grid=(steps,),
        out_shape=jax.ShapeDtypeStruct((2, beams, strip_rows, window), BF16),
        in_specs=in_specs,
        out_specs=pl.BlockSpec((2, beams, block_rows, window), lambda i: (0, 0, i + offset, 0)),
        input_output_aliases=aliases,
        scratch_shapes=[pltpu.VMEM((2 * beams * block_rows, window), F32)],
        compiler_params=pltpu.CompilerParams(vmem_limit_bytes=48 << 20),
        cost_estimate=pl.CostEstimate(
            flops=2 * matrix.size * chunk_rows * window,
            bytes_accessed=4 * beams * chunk_rows * window + 2 * matrix.shape[1] * chunk_rows * window,
            transcendentals=0,
        ),
    )(*operands)


def three_products(left_high, left_low, right_high, right_low):
    total = jnp.dot(left_low, right_high, preferred_element_type=F32)
    total += jnp.dot(left_high, right_low, preferred_element_type=F32)
    return total + jnp.dot(left_high, right_high, preferred_element_type=F32)


def residual_kernel(where_ref, live_ref, tables_ref, measured_ref, *refs):
    count = (len(refs) - 2) // 2
    block_refs, out_refs = refs[:count], refs[count : 2 * count]
    waves, backs = refs[-2:]
    chunk_rows, group, window = block_refs[0].shape
    share = group // 2
    some = chunk_rows * share

    def by_columns(high, low, table):
        return three_products(high, low, tables_ref[table], tables_ref[table + 1])

    for at, block_ref in enumerate(block_refs):
        block = block_ref[...]
        wide = jnp.concatenate(
            [block[:, :share].reshape(some, window), block[:, share:].reshape(some, window)], axis=1
        )
        high, low = split_two(wide)
        done = by_columns(high, low, 0)
        for c in range(2):
            waves[c, at * some : (at + 1) * some, :] = done[:, c * window : (c + 1) * window]

    for p in range(0, share, 2):
        columns = []
        for k in range(2):
            columns.append(
                jnp.concatenate(
                    [waves[c, pl.ds(p + k, window, stride=share), :] for c in range(2)], axis=0
                )
            )
        high, low = split_two(jnp.concatenate(columns, axis=1))
        far = three_products(tables_ref[4], tables_ref[5], high, low)
        far_re, far_im = far[:window], far[window:]
        measured = jnp.concatenate([measured_ref[p], measured_ref[p + 1]], axis=1)
        modulus = jnp.sqrt(far_re * far_re + far_im * far_im + ETA)
        keep_share = 1.0 - measured / modulus
        high, low = split_two(jnp.concatenate([far_re * keep_share, far_im * keep_share], axis=0))
        back = three_products(tables_ref[6], tables_ref[7], high, low)
        for k in range(2):
            for c in range(2):
                backs[c, pl.ds(p + k, window, stride=share), :] = back[
                    c * window : (c + 1) * window, k * window : (k + 1) * window
                ]

    for at, out_ref in enumerate(out_refs):
        wide = jnp.concatenate([backs[c, at * some : (at + 1) * some, :] for c in range(2)], axis=1)
        high, low = split_two(wide)
        done = by_columns(high, low, 2)
        for c in range(2):
            piece = done[:, c * window : (c + 1) * window].reshape(chunk_rows, share, window)
            piece = piece * live_ref[...][None]
            out_ref[:, c * share : (c + 1) * share, :] = piece.astype(BF16)


def residual(where, near_parts, far_parts, live, tables, amplitude):
    chunk_rows, group, window = near_parts[0].shape
    share = group // 2
    blocks = near_parts + far_parts
    whole = pl.BlockSpec(blocks[0].shape, lambda i, w: (0, 0, 0))
    outs = pl.pallas_call(
        residual_kernel,
        grid_spec=pltpu.PrefetchScalarGridSpec(
            num_scalar_prefetch=1,
            grid=(1,),
            in_specs=[
                pl.BlockSpec(live.shape, lambda i, w: (0, 0)),
                pl.BlockSpec(tables.shape, lambda i, w: (0, 0, 0)),
                pl.BlockSpec((share, window, window), lambda i, w: (w[0], 0, 0)),
            ]
            + [whole] * len(blocks),
            out_specs=[whole] * len(blocks),
            scratch_shapes=[
                pltpu.VMEM((2, window * share, window), F32),
                pltpu.VMEM((2, window * share, window), F32),
            ],
        ),
        out_shape=[jax.ShapeDtypeStruct(blocks[0].shape, BF16)] * len(blocks),
        compiler_params=pltpu.CompilerParams(vmem_limit_bytes=48 << 20),
        cost_estimate=pl.CostEstimate(
            flops=24 * share * 4 * window**3 * 2,
            bytes_accessed=16 * share * window * window,
            transcendentals=0,
        ),
    )(where, live, tables, amplitude, *blocks)
    return outs[: len(near_parts)], outs[len(near_parts) :]


def transform_tables(window):
    table_re, table_im = dft_tables(window)
    stacked = []
    for left in (False, True):
        for sign in (1.0, -1.0):
            imag = sign * table_im
            if left:
                top, bottom = [table_re, -imag], [imag, table_re]
            else:
                top, bottom = [table_re, imag], [-imag, table_re]
            full = jnp.concatenate(
                [jnp.concatenate(top, axis=1), jnp.concatenate(bottom, axis=1)], axis=0
            )
            stacked += list(split_two(full))
    return jnp.stack(stacked)


def share_order(shares):
    order = [0]
    bit = shares // 2
    while bit:
        order = order + [o | bit for o in order]
        bit //= 2
    return order


def body(smatrix, beam_freq, beam_amp, row_offset, col_offset, counts, amplitude):
    beam_dev = smatrix.shape[1]
    strip_rows = smatrix.shape[2]
    window = smatrix.shape[3]
    per_tile = row_offset.shape[0]
    scan_size = lax.axis_size("scan")
    shares = lax.axis_size("beam")
    share_rows = per_tile // shares
    field_rows = strip_rows * scan_size
    assert window == 2 * strip_rows
    my_tile = lax.axis_index("scan")
    my_beam = lax.axis_index("beam")
    order = share_order(shares)

    offsets = jnp.stack([row_offset, col_offset])
    offset_sets = [offsets] + [passed_along(offsets, "scan", d) for d in (1, 2)]
    stacked = jnp.stack(offset_sets).reshape(3, 2, shares, share_rows)
    stacked = jnp.take(stacked, jnp.array(order, jnp.int32) ^ my_beam, axis=2)
    rows = stacked[:, 0]
    cols = stacked[:, 1]
    distance = jnp.arange(3, dtype=jnp.int32)[:, None, None]
    tile_ids = (my_tile - distance) % scan_size
    coef_re, coef_im = coefficients(
        (tile_ids * strip_rows + rows).reshape(-1),
        cols.reshape(-1),
        beam_freq,
        beam_amp,
        field_rows,
        window,
    )
    real_rows = jnp.concatenate([coef_re, -coef_im], axis=1)
    imag_rows = jnp.concatenate([coef_im, coef_re], axis=1)
    matrix = jnp.stack(
        [
            real_rows.reshape(3 * shares, share_rows, 2 * beam_dev),
            imag_rows.reshape(3 * shares, share_rows, 2 * beam_dev),
        ],
        axis=1,
    ).reshape(6 * per_tile, 2 * beam_dev)
    low = jnp.where(distance == 0, rows, 0)
    high = jnp.where(distance == 2, rows, strip_rows)
    bounds = jnp.stack([low, high])[:, :, :, None, :]
    bounds = jnp.broadcast_to(bounds, (2, 3, shares, 2, share_rows)).reshape(2, 6 * per_tile, 1)
    bounds = jnp.broadcast_to(bounds, (2, 6 * per_tile, window))
    first_row = my_beam * share_rows
    live = (first_row + jnp.arange(share_rows, dtype=jnp.int32) < counts[0]).astype(F32)
    live = jnp.broadcast_to(live[:, None], (share_rows, window))
    tables = transform_tables(window)

    near_parts, far_parts = [], []
    largest = 0.1875 * 6.0 * 2.0 * beam_dev * shares
    scale = 2.0 ** math.floor(math.log2(60000.0 / largest))
    chunk_rows = strip_rows // CHUNKS
    for chunk in range(CHUNKS):
        kept, sent = forward(matrix, bounds, smatrix, shares, chunk, chunk_rows)
        bit = 1
        back = 1.0
        while True:
            moved = swapped(sent, "beam", bit).astype(F32) * back
            bit *= 2
            if bit == shares:
                break
            half = kept.shape[0] // 2
            sent = ((kept[half:] + moved[half:]) * scale).astype(LINK)
            back = 1.0 / scale
            kept = kept[:half] + moved[:half]
        total = kept[0] + moved[0]
        scaled = (total * scale).astype(LINK)
        second = passed_along(scaled[2], "scan", -2)
        first = passed_along(scaled[1], "scan", -1)
        near_parts.append(total[0] + second.astype(F32) / scale)
        far_parts.append(first.astype(F32) / scale)
    near_list, far_list = residual(
        my_beam.reshape(1),
        near_parts,
        far_parts,
        live,
        tables,
        amplitude,
    )
    result = None
    for chunk in range(CHUNKS):
        near, far = near_list[chunk], far_list[chunk]
        later = jnp.stack([passed_along(far, "scan", 1), passed_along(near, "scan", 2)])
        parts = []
        for strip in (near[None], later):
            held = [strip]
            bit = shares // 2
            while bit:
                held = held + [swapped(h, "beam", bit) for h in held]
                bit //= 2
            parts += held
        result = backward(
            matrix.T, bounds, parts, shares, beam_dev, strip_rows, chunk, result
        )
    return result


def solution(mesh):
    return jax.shard_map(
        body,
        mesh=mesh,
        in_specs=(
            P(None, "beam", "scan", None),
            P(None, "beam"),
            P(None, "beam"),
            P("scan"),
            P("scan"),
            P("scan"),
            P("scan", None, None),
        ),
        out_specs=P(None, "beam", "scan", None),
        check_vma=False,
    )
```

```python
import functools

import jax
import jax.numpy as jnp
import numpy as np
from jax import lax
from jax.experimental import pallas as pl
from jax.experimental.pallas import tpu as pltpu
from jax.sharding import PartitionSpec as P

TWO_PI = 6.283185307179586
ETA = 0.1
F32 = jnp.float32
BF16 = jnp.bfloat16


def passed_along(value, axis, by):
    devices = lax.axis_size(axis)
    return lax.ppermute(value, axis, [(i, (i + by) % devices) for i in range(devices)])


def swapped(value, axis, bit):
    devices = lax.axis_size(axis)
    return lax.ppermute(value, axis, [(i, i ^ bit) for i in range(devices)])


def coefficients(
    global_rows, tile_cols, beam_freq, beam_amp, field_rows, window
):
    along_rows = beam_freq[0][None, :] * global_rows[:, None] % field_rows
    along_cols = beam_freq[1][None, :] * tile_cols[:, None] % window
    phase_turns = along_rows.astype(F32) / field_rows + along_cols.astype(F32) / window
    phase_angle = -TWO_PI * phase_turns
    cos_part = jnp.cos(phase_angle)
    sin_part = jnp.sin(phase_angle)
    coef_re = beam_amp[0][None, :] * cos_part - beam_amp[1][None, :] * sin_part
    coef_im = beam_amp[0][None, :] * sin_part + beam_amp[1][None, :] * cos_part
    return (coef_re.astype(BF16), coef_im.astype(BF16))


def split_two(value):
    high = value.astype(BF16)
    return high, (value - high.astype(F32)).astype(BF16)


def forward_kernel(shares, kept, block_rows, bounds_ref, matrix_ref, strip_ref, *refs):
    outs, wide = refs[:-1], refs[-1]
    depth = matrix_ref.shape[1]
    window = strip_ref.shape[3]
    group = matrix_ref.shape[0] // (3 * shares)
    wide[...] = strip_ref[...].reshape(depth * block_rows, window).astype(F32)
    first = pl.program_id(0) * block_rows
    low = bounds_ref[0]
    high = bounds_ref[1]
    for row in range(0, block_rows, 2):
        rhs = jnp.concatenate(
            [wide[pl.ds(row + k, depth, stride=block_rows), :] for k in range(2)], axis=1
        ).astype(BF16)
        sums = jnp.dot(matrix_ref[...], rhs, preferred_element_type=F32)
        for k in range(2):
            here = first + row + k
            inside = (low <= here) & (here < high)
            part = jnp.where(inside, sums[:, k * window : (k + 1) * window], 0.0)
            for distance in range(3):
                for share in range(shares):
                    at = (distance * shares + share) * group
                    piece = part[at : at + group]
                    if share < kept:
                        outs[2 * distance][share, row + k] = piece
                    else:
                        outs[2 * distance + 1][share - kept, row + k] = piece.astype(BF16)


def forward(matrix, bounds, strip, shares, block_rows=16):
    _, beams, strip_rows, window = strip.shape
    kept = shares // 2
    group = matrix.shape[0] // (3 * shares)
    out_shape, out_specs = [], []
    for _ in range(3):
        for dtype in (F32, BF16):
            out_shape.append(jax.ShapeDtypeStruct((kept, strip_rows, group, window), dtype))
            out_specs.append(pl.BlockSpec((kept, block_rows, group, window), lambda i: (0, i, 0, 0)))
    return pl.pallas_call(
        functools.partial(forward_kernel, shares, kept, block_rows),
        grid=(strip_rows // block_rows,),
        out_shape=out_shape,
        in_specs=[
            pl.BlockSpec(bounds.shape, lambda i: (0, 0, 0)),
            pl.BlockSpec(matrix.shape, lambda i: (0, 0)),
            pl.BlockSpec((2, beams, block_rows, window), lambda i: (0, 0, i, 0)),
        ],
        out_specs=out_specs,
        scratch_shapes=[pltpu.VMEM((2 * beams * block_rows, window), F32)],
        compiler_params=pltpu.CompilerParams(vmem_limit_bytes=48 << 20),
        cost_estimate=pl.CostEstimate(
            flops=2 * matrix.size * strip_rows * window,
            bytes_accessed=2 * strip.size + 6 * matrix.shape[0] * strip_rows * window // 2,
            transcendentals=0,
        ),
    )(bounds, matrix, strip)


def backward_kernel(shares, block_rows, bounds_ref, matrix_ref, *refs):
    parts, out_ref, wide = refs[:-2], refs[-2], refs[-1]
    depth = matrix_ref.shape[0]
    window = out_ref.shape[3]
    first = pl.program_id(0) * block_rows
    low = bounds_ref[0]
    high = bounds_ref[1]
    for row in range(0, block_rows, 2):
        sides = []
        for k in range(2):
            here = first + row + k
            inside = (low <= here) & (here < high)
            tall = jnp.concatenate([part[row + k] for part in parts], axis=0)
            sides.append(jnp.where(inside, tall.astype(F32), 0.0).astype(BF16))
        sums = jnp.dot(
            matrix_ref[...], jnp.concatenate(sides, axis=1), preferred_element_type=F32
        )
        for k in range(2):
            wide[pl.ds(row + k, depth, stride=block_rows), :] = sums[:, k * window : (k + 1) * window]
    out_ref[...] = wide[...].reshape(out_ref.shape).astype(BF16)


def backward(matrix, bounds, parts, shares, beams, block_rows=16):
    strip_rows, group, window = parts[0].shape
    return pl.pallas_call(
        functools.partial(backward_kernel, shares, block_rows),
        grid=(strip_rows // block_rows,),
        out_shape=jax.ShapeDtypeStruct((2, beams, strip_rows, window), BF16),
        in_specs=[
            pl.BlockSpec(bounds.shape, lambda i: (0, 0, 0)),
            pl.BlockSpec(matrix.shape, lambda i: (0, 0)),
        ]
        + [pl.BlockSpec((block_rows, group, window), lambda i: (i, 0, 0))] * len(parts),
        out_specs=pl.BlockSpec((2, beams, block_rows, window), lambda i: (0, 0, i, 0)),
        scratch_shapes=[pltpu.VMEM((2 * beams * block_rows, window), F32)],
        compiler_params=pltpu.CompilerParams(vmem_limit_bytes=48 << 20),
        cost_estimate=pl.CostEstimate(
            flops=2 * matrix.size * strip_rows * window,
            bytes_accessed=4 * beams * strip_rows * window + 2 * len(parts) * parts[0].size,
            transcendentals=0,
        ),
    )(bounds, matrix, *parts)


def three_products(left_high, left_low, right_high, right_low):
    total = jnp.dot(left_low, right_high, preferred_element_type=F32)
    total += jnp.dot(left_high, right_low, preferred_element_type=F32)
    return total + jnp.dot(left_high, right_high, preferred_element_type=F32)


def residual_kernel(where_ref, first_ref, second_ref, third_ref, fourth_ref, live_ref, tables_ref,
                    measured_ref, low_ref, high_ref, waves, backs):
    strip_rows, group, window = first_ref.shape
    share = group // 2
    rows = strip_rows * share

    def by_columns(high, low, table):
        return three_products(high, low, tables_ref[table], tables_ref[table + 1])

    for half in range(2):
        if half == 0:
            block = first_ref[...] + second_ref[...].astype(F32) + fourth_ref[...].astype(F32)
        else:
            block = third_ref[...].astype(F32)
        wide = jnp.concatenate(
            [block[:, :share].reshape(rows, window), block[:, share:].reshape(rows, window)], axis=1
        )
        high, low = split_two(wide)
        done = by_columns(high, low, 0)
        for c in range(2):
            waves[c, half * rows : (half + 1) * rows, :] = done[:, c * window : (c + 1) * window]

    for p in range(0, share, 2):
        columns = []
        for k in range(2):
            columns.append(
                jnp.concatenate(
                    [waves[c, pl.ds(p + k, window, stride=share), :] for c in range(2)], axis=0
                )
            )
        high, low = split_two(jnp.concatenate(columns, axis=1))
        far = three_products(tables_ref[4], tables_ref[5], high, low)
        far_re, far_im = far[:window], far[window:]
        measured = jnp.concatenate([measured_ref[p], measured_ref[p + 1]], axis=1)
        modulus = jnp.sqrt(far_re * far_re + far_im * far_im + ETA)
        keep_share = 1.0 - measured / modulus
        high, low = split_two(jnp.concatenate([far_re * keep_share, far_im * keep_share], axis=0))
        back = three_products(tables_ref[6], tables_ref[7], high, low)
        for k in range(2):
            for c in range(2):
                backs[c, pl.ds(p + k, window, stride=share), :] = back[
                    c * window : (c + 1) * window, k * window : (k + 1) * window
                ]

    for half, out_ref in ((0, low_ref), (1, high_ref)):
        wide = jnp.concatenate(
            [backs[c, half * rows : (half + 1) * rows, :] for c in range(2)], axis=1
        )
        high, low = split_two(wide)
        done = by_columns(high, low, 2)
        for c in range(2):
            piece = done[:, c * window : (c + 1) * window].reshape(strip_rows, share, window)
            piece = piece * live_ref[...][None]
            out_ref[:, c * share : (c + 1) * share, :] = piece.astype(BF16)


def residual(where, first, second, third, fourth, live, tables, amplitude):
    strip_rows, group, window = first.shape
    share = group // 2
    whole = pl.BlockSpec(first.shape, lambda i, w: (0, 0, 0))
    return pl.pallas_call(
        residual_kernel,
        grid_spec=pltpu.PrefetchScalarGridSpec(
            num_scalar_prefetch=1,
            grid=(1,),
            in_specs=[
                whole,
                whole,
                whole,
                whole,
                pl.BlockSpec(live.shape, lambda i, w: (0, 0)),
                pl.BlockSpec(tables.shape, lambda i, w: (0, 0, 0)),
                pl.BlockSpec((share, window, window), lambda i, w: (w[0], 0, 0)),
            ],
            out_specs=[whole, whole],
            scratch_shapes=[
                pltpu.VMEM((2, window * share, window), F32),
                pltpu.VMEM((2, window * share, window), F32),
            ],
        ),
        out_shape=[jax.ShapeDtypeStruct(first.shape, BF16)] * 2,
        compiler_params=pltpu.CompilerParams(vmem_limit_bytes=48 << 20),
        cost_estimate=pl.CostEstimate(
            flops=24 * share * 4 * window**3 * 2,
            bytes_accessed=16 * first.size,
            transcendentals=0,
        ),
    )(where, first, second, third, fourth, live, tables, amplitude)


def transform_tables(window):
    counter = np.arange(window)
    turn_angle = (counter[:, None] * counter[None, :] % window) * (2.0 * np.pi / window)
    table_re = np.cos(turn_angle) / np.sqrt(window)
    table_im = -np.sin(turn_angle) / np.sqrt(window)
    stacked = []
    for left in (False, True):
        for sign in (1.0, -1.0):
            imag = sign * table_im
            if left:
                full = np.block([[table_re, -imag], [imag, table_re]])
            else:
                full = np.block([[table_re, imag], [-imag, table_re]])
            high = full.astype(BF16)
            stacked += [high, (full - high.astype(np.float64)).astype(BF16)]
    return jnp.asarray(np.stack(stacked))


def share_order(shares):
    order = [0]
    bit = shares // 2
    while bit:
        order = order + [o | bit for o in order]
        bit //= 2
    return order


def body(smatrix, beam_freq, beam_amp, row_offset, col_offset, counts, amplitude):
    beam_dev = smatrix.shape[1]
    strip_rows = smatrix.shape[2]
    window = smatrix.shape[3]
    per_tile = row_offset.shape[0]
    scan_size = lax.axis_size("scan")
    shares = lax.axis_size("beam")
    share_rows = per_tile // shares
    field_rows = strip_rows * scan_size
    assert window == 2 * strip_rows
    my_tile = lax.axis_index("scan")
    my_beam = lax.axis_index("beam")
    order = share_order(shares)

    offsets = jnp.stack([row_offset, col_offset])
    offset_sets = [offsets] + [passed_along(offsets, "scan", d) for d in (1, 2)]
    stacked = jnp.stack(offset_sets).reshape(3, 2, shares, share_rows)
    stacked = jnp.take(stacked, jnp.array(order, jnp.int32) ^ my_beam, axis=2)
    rows = stacked[:, 0]
    cols = stacked[:, 1]
    distance = jnp.arange(3, dtype=jnp.int32)[:, None, None]
    tile_ids = (my_tile - distance) % scan_size
    coef_re, coef_im = coefficients(
        (tile_ids * strip_rows + rows).reshape(-1),
        cols.reshape(-1),
        beam_freq,
        beam_amp,
        field_rows,
        window,
    )
    real_rows = jnp.concatenate([coef_re, -coef_im], axis=1)
    imag_rows = jnp.concatenate([coef_im, coef_re], axis=1)
    matrix = jnp.stack(
        [
            real_rows.reshape(3 * shares, share_rows, 2 * beam_dev),
            imag_rows.reshape(3 * shares, share_rows, 2 * beam_dev),
        ],
        axis=1,
    ).reshape(6 * per_tile, 2 * beam_dev)
    low = jnp.where(distance == 0, rows, 0)
    high = jnp.where(distance == 2, rows, strip_rows)
    bounds = jnp.stack([low, high])[:, :, :, None, :]
    bounds = jnp.broadcast_to(bounds, (2, 3, shares, 2, share_rows)).reshape(2, 6 * per_tile, 1)
    bounds = jnp.broadcast_to(bounds, (2, 6 * per_tile, window))
    first_row = my_beam * share_rows
    live = (first_row + jnp.arange(share_rows, dtype=jnp.int32) < counts[0]).astype(F32)
    live = jnp.broadcast_to(live[:, None], (share_rows, window))
    tables = transform_tables(window)

    sums = forward(matrix, bounds, smatrix, shares)
    summed = [None, None, None]
    for d in (2, 1, 0):
        kept, sent = sums[2 * d], sums[2 * d + 1]
        bit = 1
        while True:
            moved = swapped(sent, "beam", bit)
            bit *= 2
            if bit == shares:
                break
            half = kept.shape[0] // 2
            sent = (kept[half:] + moved[half:].astype(F32)).astype(BF16)
            kept = kept[:half] + moved[:half].astype(F32)
        summed[d] = (kept[0], moved[0])
    shifted = {}
    for d in (2, 1):
        total = (summed[d][0] + summed[d][1].astype(F32)).astype(BF16)
        shifted[d] = passed_along(total, "scan", -d)
    near, far = residual(
        my_beam.reshape(1), summed[0][0], summed[0][1], shifted[1], shifted[2], live, tables, amplitude
    )
    strips = [near, passed_along(far, "scan", 1), passed_along(near, "scan", 2)]
    parts = []
    for strip in strips:
        held = [strip]
        bit = shares // 2
        while bit:
            held = held + [swapped(h, "beam", bit) for h in held]
            bit //= 2
        parts += held
    return backward(matrix.T, bounds, parts, shares, beam_dev)


def solution(mesh):
    return jax.shard_map(
        body,
        mesh=mesh,
        in_specs=(
            P(None, "beam", "scan", None),
            P(None, "beam"),
            P(None, "beam"),
            P("scan"),
            P("scan"),
            P("scan"),
            P("scan", None, None),
        ),
        out_specs=P(None, "beam", "scan", None),
        check_vma=False,
    )
```

```python
import functools

import jax
import jax.numpy as jnp
import numpy as np
from jax import lax
from jax.experimental import pallas as pl
from jax.experimental.pallas import tpu as pltpu
from jax.sharding import PartitionSpec as P

TWO_PI = 6.283185307179586
ETA = 0.1
F32 = jnp.float32
BF16 = jnp.bfloat16
MESH = pl.DeviceIdType.MESH


def passed_along(value, axis, by):
    devices = lax.axis_size(axis)
    return lax.ppermute(value, axis, [(i, (i + by) % devices) for i in range(devices)])


def swapped(value, axis, bit):
    devices = lax.axis_size(axis)
    return lax.ppermute(value, axis, [(i, i ^ bit) for i in range(devices)])


def coefficients(
    global_rows, tile_cols, beam_freq, beam_amp, field_rows, window
):
    along_rows = beam_freq[0][None, :] * global_rows[:, None] % field_rows
    along_cols = beam_freq[1][None, :] * tile_cols[:, None] % window
    phase_turns = along_rows.astype(F32) / field_rows + along_cols.astype(F32) / window
    phase_angle = -TWO_PI * phase_turns
    cos_part = jnp.cos(phase_angle)
    sin_part = jnp.sin(phase_angle)
    coef_re = beam_amp[0][None, :] * cos_part - beam_amp[1][None, :] * sin_part
    coef_im = beam_amp[0][None, :] * sin_part + beam_amp[1][None, :] * cos_part
    return (coef_re.astype(BF16), coef_im.astype(BF16))


def split_two(value):
    high = value.astype(BF16)
    return high, (value - high.astype(F32)).astype(BF16)


def forward_kernel(shares, scan_size, bounds_ref, matrix_ref, strip_ref, near_ref, far_ref,
                   strips, wide, kept, core_out, core_in, link_out, link_in, scan_out, scan_in,
                   load_sem, core_send, core_recv, link_send, link_recv, scan_send, scan_recv):
    chunks, pairs, _, block_rows, group, window = kept.shape
    beams = strip_ref.shape[1]
    depth = 2 * beams
    me = lax.axis_index("beam")
    tile = lax.axis_index("scan")
    core_mate = {"beam": me + 1 - 2 * lax.rem(me, 2)}
    link_mate = {"beam": lax.rem(me + shares // 2, shares)}
    owners = [{"scan": lax.rem(tile + scan_size - d, scan_size)} for d in (1, 2)]
    givers = [{"scan": lax.rem(tile + d, scan_size)} for d in (1, 2)]

    def load(chunk):
        return pltpu.make_async_copy(
            strip_ref.at[:, :, pl.ds(chunk * block_rows, block_rows), :],
            strips.at[chunk % 2],
            load_sem.at[chunk % 2],
        )

    def to_core(chunk):
        return pltpu.make_async_remote_copy(
            core_out.at[chunk], core_in.at[chunk], core_send.at[chunk], core_recv.at[chunk],
            device_id=core_mate, device_id_type=MESH,
        )

    def to_link(chunk):
        return pltpu.make_async_remote_copy(
            link_out.at[chunk], link_in.at[chunk], link_send.at[chunk], link_recv.at[chunk],
            device_id=link_mate, device_id_type=MESH,
        )

    def to_scan(chunk, which):
        return pltpu.make_async_remote_copy(
            scan_out.at[chunk, which], scan_in.at[chunk, which],
            scan_send.at[chunk, which], scan_recv.at[chunk, which],
            device_id=owners[which], device_id_type=MESH,
        )

    load(0).start()
    load(1).start()
    barrier = pltpu.get_barrier_semaphore()
    peers = [core_mate, link_mate] + owners + givers
    for peer in peers:
        pl.semaphore_signal(barrier, inc=1, device_id=peer, device_id_type=MESH)
    pl.semaphore_wait(barrier, len(peers))

    def compute(chunk):
        load(chunk).wait()
        wide[...] = strips[chunk % 2].reshape(depth * block_rows, window).astype(F32)
        if chunk + 2 < chunks:
            load(chunk + 2).start()

        def pair_of_rows(step, carry):
            row = step * 2
            rhs = jnp.concatenate(
                [wide[pl.ds(row + k, depth, stride=block_rows), :] for k in range(2)], axis=1
            ).astype(BF16)
            sums = jnp.dot(matrix_ref[...], rhs, preferred_element_type=F32)
            for k in range(2):
                here = chunk * block_rows + row + k
                inside = (bounds_ref[0] <= here) & (here < bounds_ref[1])
                part = jnp.where(inside, sums[:, k * window : (k + 1) * window], 0.0)
                for d in range(3):
                    for share in range(shares):
                        at = (d * shares + share) * group
                        piece = part[at : at + group]
                        if share < pairs:
                            kept[chunk, share, d, row + k] = piece
                        else:
                            core_out[chunk, share - pairs, d, row + k] = piece.astype(BF16)
            return carry

        lax.fori_loop(0, block_rows // 2, pair_of_rows, 0)
        to_core(chunk).start()

    def over_link(chunk):
        to_core(chunk).wait_recv()
        link_out[chunk] = (kept[chunk, 1] + core_in[chunk, 1].astype(F32)).astype(BF16)
        to_link(chunk).start()

    def over_scan(chunk):
        to_link(chunk).wait_recv()
        for d in (1, 2, 0):
            total = kept[chunk, 0, d] + core_in[chunk, 0, d].astype(F32) + link_in[chunk, d].astype(F32)
            if d:
                scan_out[chunk, d - 1] = total.astype(BF16)
                to_scan(chunk, d - 1).start()
            else:
                near_ref[chunk * block_rows : (chunk + 1) * block_rows] = total

    def finish(chunk):
        rows = slice(chunk * block_rows, (chunk + 1) * block_rows)
        to_scan(chunk, 0).wait_recv()
        far_ref[rows] = scan_in[chunk, 0].astype(F32)
        to_scan(chunk, 1).wait_recv()
        near_ref[rows] += scan_in[chunk, 1].astype(F32)

    for chunk in range(chunks):
        compute(chunk)
        if chunk:
            over_link(chunk - 1)
    over_link(chunks - 1)
    for chunk in range(chunks):
        over_scan(chunk)
    for chunk in range(chunks):
        finish(chunk)
    for chunk in range(chunks):
        to_core(chunk).wait_send()
        to_link(chunk).wait_send()
        for which in range(2):
            to_scan(chunk, which).wait_send()


def forward(matrix, bounds, strip, shares, scan_size, block_rows=16):
    _, beams, strip_rows, window = strip.shape
    assert shares == 4 and scan_size > 4
    pairs = shares // 2
    group = matrix.shape[0] // (3 * shares)
    chunks = strip_rows // block_rows
    tail = (block_rows, group, window)
    vmem = pl.BlockSpec(memory_space=pltpu.VMEM)
    dma = pltpu.SemaphoreType.DMA
    return pl.pallas_call(
        functools.partial(forward_kernel, shares, scan_size),
        out_shape=[jax.ShapeDtypeStruct((strip_rows, group, window), F32)] * 2,
        in_specs=[vmem, vmem, pl.BlockSpec(memory_space=pl.ANY)],
        out_specs=[vmem, vmem],
        scratch_shapes=[
            pltpu.VMEM((2, 2, beams, block_rows, window), BF16),
            pltpu.VMEM((2 * beams * block_rows, window), F32),
            pltpu.VMEM((chunks, pairs, 3) + tail, F32),
            pltpu.VMEM((chunks, pairs, 3) + tail, BF16),
            pltpu.VMEM((chunks, pairs, 3) + tail, BF16),
            pltpu.VMEM((chunks, 3) + tail, BF16),
            pltpu.VMEM((chunks, 3) + tail, BF16),
            pltpu.VMEM((chunks, 2) + tail, BF16),
            pltpu.VMEM((chunks, 2) + tail, BF16),
            dma((2,)),
            dma((chunks,)),
            dma((chunks,)),
            dma((chunks,)),
            dma((chunks,)),
            dma((chunks, 2)),
            dma((chunks, 2)),
        ],
        compiler_params=pltpu.CompilerParams(
            collective_id=0, has_side_effects=True, vmem_limit_bytes=52 << 20
        ),
        cost_estimate=pl.CostEstimate(
            flops=2 * matrix.size * strip_rows * window,
            bytes_accessed=4 * beams * strip_rows * window,
            transcendentals=0,
        ),
    )(bounds, matrix, strip)


def backward_kernel(shares, block_rows, bounds_ref, matrix_ref, *refs):
    parts, out_ref, wide = refs[:-2], refs[-2], refs[-1]
    depth = matrix_ref.shape[0]
    window = out_ref.shape[3]
    first = pl.program_id(0) * block_rows
    low = bounds_ref[0]
    high = bounds_ref[1]
    for row in range(0, block_rows, 2):
        sides = []
        for k in range(2):
            here = first + row + k
            inside = (low <= here) & (here < high)
            tall = jnp.concatenate([part[row + k] for part in parts], axis=0)
            sides.append(jnp.where(inside, tall.astype(F32), 0.0).astype(BF16))
        sums = jnp.dot(
            matrix_ref[...], jnp.concatenate(sides, axis=1), preferred_element_type=F32
        )
        for k in range(2):
            wide[pl.ds(row + k, depth, stride=block_rows), :] = sums[:, k * window : (k + 1) * window]
    out_ref[...] = wide[...].reshape(out_ref.shape).astype(BF16)


def backward(matrix, bounds, parts, shares, beams, block_rows=16):
    strip_rows, group, window = parts[0].shape
    return pl.pallas_call(
        functools.partial(backward_kernel, shares, block_rows),
        grid=(strip_rows // block_rows,),
        out_shape=jax.ShapeDtypeStruct((2, beams, strip_rows, window), BF16),
        in_specs=[
            pl.BlockSpec(bounds.shape, lambda i: (0, 0, 0)),
            pl.BlockSpec(matrix.shape, lambda i: (0, 0)),
        ]
        + [pl.BlockSpec((block_rows, group, window), lambda i: (i, 0, 0))] * len(parts),
        out_specs=pl.BlockSpec((2, beams, block_rows, window), lambda i: (0, 0, i, 0)),
        scratch_shapes=[pltpu.VMEM((2 * beams * block_rows, window), F32)],
        compiler_params=pltpu.CompilerParams(vmem_limit_bytes=48 << 20),
        cost_estimate=pl.CostEstimate(
            flops=2 * matrix.size * strip_rows * window,
            bytes_accessed=4 * beams * strip_rows * window + 2 * len(parts) * parts[0].size,
            transcendentals=0,
        ),
    )(bounds, matrix, *parts)


def three_products(left_high, left_low, right_high, right_low):
    total = jnp.dot(left_low, right_high, preferred_element_type=F32)
    total += jnp.dot(left_high, right_low, preferred_element_type=F32)
    return total + jnp.dot(left_high, right_high, preferred_element_type=F32)


def residual_kernel(where_ref, first_ref, second_ref, live_ref, tables_ref,
                    measured_ref, low_ref, high_ref, waves, backs):
    strip_rows, group, window = first_ref.shape
    share = group // 2
    rows = strip_rows * share

    def by_columns(high, low, table):
        return three_products(high, low, tables_ref[table], tables_ref[table + 1])

    for half in range(2):
        block = (first_ref if half == 0 else second_ref)[...]
        wide = jnp.concatenate(
            [block[:, :share].reshape(rows, window), block[:, share:].reshape(rows, window)], axis=1
        )
        high, low = split_two(wide)
        done = by_columns(high, low, 0)
        for c in range(2):
            waves[c, half * rows : (half + 1) * rows, :] = done[:, c * window : (c + 1) * window]

    for p in range(0, share, 2):
        columns = []
        for k in range(2):
            columns.append(
                jnp.concatenate(
                    [waves[c, pl.ds(p + k, window, stride=share), :] for c in range(2)], axis=0
                )
            )
        high, low = split_two(jnp.concatenate(columns, axis=1))
        far = three_products(tables_ref[4], tables_ref[5], high, low)
        far_re, far_im = far[:window], far[window:]
        measured = jnp.concatenate([measured_ref[p], measured_ref[p + 1]], axis=1)
        modulus = jnp.sqrt(far_re * far_re + far_im * far_im + ETA)
        keep_share = 1.0 - measured / modulus
        high, low = split_two(jnp.concatenate([far_re * keep_share, far_im * keep_share], axis=0))
        back = three_products(tables_ref[6], tables_ref[7], high, low)
        for k in range(2):
            for c in range(2):
                backs[c, pl.ds(p + k, window, stride=share), :] = back[
                    c * window : (c + 1) * window, k * window : (k + 1) * window
                ]

    for half, out_ref in ((0, low_ref), (1, high_ref)):
        wide = jnp.concatenate(
            [backs[c, half * rows : (half + 1) * rows, :] for c in range(2)], axis=1
        )
        high, low = split_two(wide)
        done = by_columns(high, low, 2)
        for c in range(2):
            piece = done[:, c * window : (c + 1) * window].reshape(strip_rows, share, window)
            piece = piece * live_ref[...][None]
            out_ref[:, c * share : (c + 1) * share, :] = piece.astype(BF16)


def residual(where, first, second, live, tables, amplitude):
    strip_rows, group, window = first.shape
    share = group // 2
    whole = pl.BlockSpec(first.shape, lambda i, w: (0, 0, 0))
    return pl.pallas_call(
        residual_kernel,
        grid_spec=pltpu.PrefetchScalarGridSpec(
            num_scalar_prefetch=1,
            grid=(1,),
            in_specs=[
                whole,
                whole,
                pl.BlockSpec(live.shape, lambda i, w: (0, 0)),
                pl.BlockSpec(tables.shape, lambda i, w: (0, 0, 0)),
                pl.BlockSpec((share, window, window), lambda i, w: (w[0], 0, 0)),
            ],
            out_specs=[whole, whole],
            scratch_shapes=[
                pltpu.VMEM((2, window * share, window), F32),
                pltpu.VMEM((2, window * share, window), F32),
            ],
        ),
        out_shape=[jax.ShapeDtypeStruct(first.shape, BF16)] * 2,
        compiler_params=pltpu.CompilerParams(vmem_limit_bytes=48 << 20),
        cost_estimate=pl.CostEstimate(
            flops=24 * share * 4 * window**3 * 2,
            bytes_accessed=16 * first.size,
            transcendentals=0,
        ),
    )(where, first, second, live, tables, amplitude)


def transform_tables(window):
    counter = np.arange(window)
    turn_angle = (counter[:, None] * counter[None, :] % window) * (2.0 * np.pi / window)
    table_re = np.cos(turn_angle) / np.sqrt(window)
    table_im = -np.sin(turn_angle) / np.sqrt(window)
    stacked = []
    for left in (False, True):
        for sign in (1.0, -1.0):
            imag = sign * table_im
            if left:
                full = np.block([[table_re, -imag], [imag, table_re]])
            else:
                full = np.block([[table_re, imag], [-imag, table_re]])
            high = full.astype(BF16)
            stacked += [high, (full - high.astype(np.float64)).astype(BF16)]
    return jnp.asarray(np.stack(stacked))


def share_order(shares):
    order = [0]
    bit = shares // 2
    while bit:
        order = order + [o | bit for o in order]
        bit //= 2
    return order


def body(smatrix, beam_freq, beam_amp, row_offset, col_offset, counts, amplitude):
    beam_dev = smatrix.shape[1]
    strip_rows = smatrix.shape[2]
    window = smatrix.shape[3]
    per_tile = row_offset.shape[0]
    scan_size = lax.axis_size("scan")
    shares = lax.axis_size("beam")
    share_rows = per_tile // shares
    field_rows = strip_rows * scan_size
    assert window == 2 * strip_rows
    my_tile = lax.axis_index("scan")
    my_beam = lax.axis_index("beam")
    order = share_order(shares)

    offsets = jnp.stack([row_offset, col_offset])
    offset_sets = [offsets] + [passed_along(offsets, "scan", d) for d in (1, 2)]
    stacked = jnp.stack(offset_sets).reshape(3, 2, shares, share_rows)
    stacked = jnp.take(stacked, jnp.array(order, jnp.int32) ^ my_beam, axis=2)
    rows = stacked[:, 0]
    cols = stacked[:, 1]
    distance = jnp.arange(3, dtype=jnp.int32)[:, None, None]
    tile_ids = (my_tile - distance) % scan_size
    coef_re, coef_im = coefficients(
        (tile_ids * strip_rows + rows).reshape(-1),
        cols.reshape(-1),
        beam_freq,
        beam_amp,
        field_rows,
        window,
    )
    real_rows = jnp.concatenate([coef_re, -coef_im], axis=1)
    imag_rows = jnp.concatenate([coef_im, coef_re], axis=1)
    matrix = jnp.stack(
        [
            real_rows.reshape(3 * shares, share_rows, 2 * beam_dev),
            imag_rows.reshape(3 * shares, share_rows, 2 * beam_dev),
        ],
        axis=1,
    ).reshape(6 * per_tile, 2 * beam_dev)
    low = jnp.where(distance == 0, rows, 0)
    high = jnp.where(distance == 2, rows, strip_rows)
    bounds = jnp.stack([low, high])[:, :, :, None, :]
    bounds = jnp.broadcast_to(bounds, (2, 3, shares, 2, share_rows)).reshape(2, 6 * per_tile, 1)
    bounds = jnp.broadcast_to(bounds, (2, 6 * per_tile, window))
    first_row = my_beam * share_rows
    live = (first_row + jnp.arange(share_rows, dtype=jnp.int32) < counts[0]).astype(F32)
    live = jnp.broadcast_to(live[:, None], (share_rows, window))
    tables = transform_tables(window)

    near, far = forward(matrix, bounds, smatrix, shares, scan_size)
    near, far = residual(my_beam.reshape(1), near, far, live, tables, amplitude)
    strips = [near, passed_along(far, "scan", 1), passed_along(near, "scan", 2)]
    parts = []
    for strip in strips:
        held = [strip]
        bit = shares // 2
        while bit:
            held = held + [swapped(h, "beam", bit) for h in held]
            bit //= 2
        parts += held
    return backward(matrix.T, bounds, parts, shares, beam_dev)


def solution(mesh):
    return jax.shard_map(
        body,
        mesh=mesh,
        in_specs=(
            P(None, "beam", "scan", None),
            P(None, "beam"),
            P(None, "beam"),
            P("scan"),
            P("scan"),
            P("scan"),
            P("scan", None, None),
        ),
        out_specs=P(None, "beam", "scan", None),
        check_vma=False,
    )
```

```python
import functools

import jax
import jax.numpy as jnp
import numpy as np
from jax import lax
from jax.experimental import pallas as pl
from jax.experimental.pallas import tpu as pltpu
from jax.sharding import PartitionSpec as P

TWO_PI = 6.283185307179586
ETA = 0.1
F32 = jnp.float32
BF16 = jnp.bfloat16
MESH = pl.DeviceIdType.MESH


def passed_along(value, axis, by):
    devices = lax.axis_size(axis)
    return lax.ppermute(value, axis, [(i, (i + by) % devices) for i in range(devices)])


def swapped(value, axis, bit):
    devices = lax.axis_size(axis)
    return lax.ppermute(value, axis, [(i, i ^ bit) for i in range(devices)])


def coefficients(
    global_rows, tile_cols, beam_freq, beam_amp, field_rows, window
):
    along_rows = beam_freq[0][None, :] * global_rows[:, None] % field_rows
    along_cols = beam_freq[1][None, :] * tile_cols[:, None] % window
    phase_turns = along_rows.astype(F32) / field_rows + along_cols.astype(F32) / window
    phase_angle = -TWO_PI * phase_turns
    cos_part = jnp.cos(phase_angle)
    sin_part = jnp.sin(phase_angle)
    coef_re = beam_amp[0][None, :] * cos_part - beam_amp[1][None, :] * sin_part
    coef_im = beam_amp[0][None, :] * sin_part + beam_amp[1][None, :] * cos_part
    return (coef_re.astype(BF16), coef_im.astype(BF16))


def split_two(value):
    high = value.astype(BF16)
    return high, (value - high.astype(F32)).astype(BF16)


def forward_kernel(shares, scan_size, bounds_ref, matrix_ref, strip_ref, near_ref, far_ref,
                   strips, wide, kept, core_out, core_in, link_out, link_in, scan_out, scan_in,
                   load_sem, core_send, core_recv, link_send, link_recv, scan_send, scan_recv):
    chunks, pairs, _, block_rows, group, window = kept.shape
    beams = strip_ref.shape[1]
    depth = 2 * beams
    me = lax.axis_index("beam")
    tile = lax.axis_index("scan")
    core_mate = {"beam": me + 1 - 2 * lax.rem(me, 2)}
    link_mate = {"beam": lax.rem(me + shares // 2, shares)}
    owners = [{"scan": lax.rem(tile + scan_size - d, scan_size)} for d in (1, 2)]
    givers = [{"scan": lax.rem(tile + d, scan_size)} for d in (1, 2)]

    def load(chunk):
        return pltpu.make_async_copy(
            strip_ref.at[:, :, pl.ds(chunk * block_rows, block_rows), :],
            strips.at[chunk % 2],
            load_sem.at[chunk % 2],
        )

    def to_core(chunk):
        return pltpu.make_async_remote_copy(
            core_out.at[chunk], core_in.at[chunk], core_send.at[chunk], core_recv.at[chunk],
            device_id=core_mate, device_id_type=MESH,
        )

    def to_link(chunk):
        return pltpu.make_async_remote_copy(
            link_out.at[chunk], link_in.at[chunk], link_send.at[chunk], link_recv.at[chunk],
            device_id=link_mate, device_id_type=MESH,
        )

    def to_scan(chunk, which):
        return pltpu.make_async_remote_copy(
            scan_out.at[chunk, which], scan_in.at[chunk, which],
            scan_send.at[chunk, which], scan_recv.at[chunk, which],
            device_id=owners[which], device_id_type=MESH,
        )

    load(0).start()
    load(1).start()
    barrier = pltpu.get_barrier_semaphore()
    peers = [core_mate, link_mate] + owners + givers
    for peer in peers:
        pl.semaphore_signal(barrier, inc=1, device_id=peer, device_id_type=MESH)
    pl.semaphore_wait(barrier, len(peers))

    def compute(chunk):
        load(chunk).wait()
        wide[...] = strips[chunk % 2].astype(F32).reshape(depth * block_rows, window)
        if chunk + 2 < chunks:
            load(chunk + 2).start()

        def pair_of_rows(step, carry):
            row = step * 2
            rhs = jnp.concatenate(
                [wide[pl.ds(row + k, depth, stride=block_rows), :] for k in range(2)], axis=1
            ).astype(BF16)
            sums = jnp.dot(matrix_ref[...], rhs, preferred_element_type=F32)
            for k in range(2):
                here = chunk * block_rows + row + k
                inside = (bounds_ref[0] <= here) & (here < bounds_ref[1])
                part = jnp.where(inside, sums[:, k * window : (k + 1) * window], 0.0)
                for d in range(3):
                    for share in range(shares):
                        at = (d * shares + share) * group
                        piece = part[at : at + group]
                        if share < pairs:
                            kept[chunk, share, d, row + k] = piece
                        else:
                            core_out[chunk, share - pairs, d, row + k] = piece.astype(BF16)
            return carry

        lax.fori_loop(0, block_rows // 2, pair_of_rows, 0)
        to_core(chunk).start()

    def over_link(chunk):
        to_core(chunk).wait_recv()
        link_out[chunk] = (kept[chunk, 1] + core_in[chunk, 1].astype(F32)).astype(BF16)
        to_link(chunk).start()

    def over_scan(chunk):
        to_link(chunk).wait_recv()
        for d in (1, 2, 0):
            total = kept[chunk, 0, d] + core_in[chunk, 0, d].astype(F32) + link_in[chunk, d].astype(F32)
            if d:
                scan_out[chunk, d - 1] = total.astype(BF16)
                to_scan(chunk, d - 1).start()
            else:
                near_ref[chunk * block_rows : (chunk + 1) * block_rows] = total

    def finish(chunk):
        rows = slice(chunk * block_rows, (chunk + 1) * block_rows)
        to_scan(chunk, 0).wait_recv()
        far_ref[rows] = scan_in[chunk, 0].astype(F32)
        to_scan(chunk, 1).wait_recv()
        near_ref[rows] += scan_in[chunk, 1].astype(F32)

    for chunk in range(chunks):
        compute(chunk)
        if chunk:
            over_link(chunk - 1)
    over_link(chunks - 1)
    for chunk in range(chunks):
        over_scan(chunk)
    for chunk in range(chunks):
        finish(chunk)
    for chunk in range(chunks):
        to_core(chunk).wait_send()
        to_link(chunk).wait_send()
        for which in range(2):
            to_scan(chunk, which).wait_send()


def forward(matrix, bounds, strip, shares, scan_size, block_rows=8):
    _, beams, strip_rows, window = strip.shape
    assert shares == 4 and scan_size > 4
    pairs = shares // 2
    group = matrix.shape[0] // (3 * shares)
    chunks = strip_rows // block_rows
    tail = (block_rows, group, window)
    vmem = pl.BlockSpec(memory_space=pltpu.VMEM)
    dma = pltpu.SemaphoreType.DMA
    return pl.pallas_call(
        functools.partial(forward_kernel, shares, scan_size),
        out_shape=[jax.ShapeDtypeStruct((strip_rows, group, window), F32)] * 2,
        in_specs=[vmem, vmem, pl.BlockSpec(memory_space=pl.ANY)],
        out_specs=[vmem, vmem],
        scratch_shapes=[
            pltpu.VMEM((2, 2, beams, block_rows, window), BF16),
            pltpu.VMEM((2 * beams * block_rows, window), F32),
            pltpu.VMEM((chunks, pairs, 3) + tail, F32),
            pltpu.VMEM((chunks, pairs, 3) + tail, BF16),
            pltpu.VMEM((chunks, pairs, 3) + tail, BF16),
            pltpu.VMEM((chunks, 3) + tail, BF16),
            pltpu.VMEM((chunks, 3) + tail, BF16),
            pltpu.VMEM((chunks, 2) + tail, BF16),
            pltpu.VMEM((chunks, 2) + tail, BF16),
            dma((2,)),
            dma((chunks,)),
            dma((chunks,)),
            dma((chunks,)),
            dma((chunks,)),
            dma((chunks, 2)),
            dma((chunks, 2)),
        ],
        compiler_params=pltpu.CompilerParams(
            collective_id=0, has_side_effects=True, vmem_limit_bytes=52 << 20
        ),
        cost_estimate=pl.CostEstimate(
            flops=2 * matrix.size * strip_rows * window,
            bytes_accessed=4 * beams * strip_rows * window,
            transcendentals=0,
        ),
    )(bounds, matrix, strip)


def backward_kernel(shares, block_rows, bounds_ref, matrix_ref, *refs):
    parts, out_ref, wide = refs[:-2], refs[-2], refs[-1]
    depth = matrix_ref.shape[0]
    window = out_ref.shape[3]
    first = pl.program_id(0) * block_rows
    low = bounds_ref[0]
    high = bounds_ref[1]
    for row in range(0, block_rows, 2):
        sides = []
        for k in range(2):
            here = first + row + k
            inside = (low <= here) & (here < high)
            tall = jnp.concatenate([part[row + k] for part in parts], axis=0)
            sides.append(jnp.where(inside, tall.astype(F32), 0.0).astype(BF16))
        sums = jnp.dot(
            matrix_ref[...], jnp.concatenate(sides, axis=1), preferred_element_type=F32
        )
        for k in range(2):
            wide[pl.ds(row + k, depth, stride=block_rows), :] = sums[:, k * window : (k + 1) * window]
    out_ref[...] = wide[...].reshape(out_ref.shape).astype(BF16)


def backward(matrix, bounds, parts, shares, beams, block_rows=16):
    strip_rows, group, window = parts[0].shape
    return pl.pallas_call(
        functools.partial(backward_kernel, shares, block_rows),
        grid=(strip_rows // block_rows,),
        out_shape=jax.ShapeDtypeStruct((2, beams, strip_rows, window), BF16),
        in_specs=[
            pl.BlockSpec(bounds.shape, lambda i: (0, 0, 0)),
            pl.BlockSpec(matrix.shape, lambda i: (0, 0)),
        ]
        + [pl.BlockSpec((block_rows, group, window), lambda i: (i, 0, 0))] * len(parts),
        out_specs=pl.BlockSpec((2, beams, block_rows, window), lambda i: (0, 0, i, 0)),
        scratch_shapes=[pltpu.VMEM((2 * beams * block_rows, window), F32)],
        compiler_params=pltpu.CompilerParams(vmem_limit_bytes=48 << 20),
        cost_estimate=pl.CostEstimate(
            flops=2 * matrix.size * strip_rows * window,
            bytes_accessed=4 * beams * strip_rows * window + 2 * len(parts) * parts[0].size,
            transcendentals=0,
        ),
    )(bounds, matrix, *parts)


def three_products(left_high, left_low, right_high, right_low):
    total = jnp.dot(left_low, right_high, preferred_element_type=F32)
    total += jnp.dot(left_high, right_low, preferred_element_type=F32)
    return total + jnp.dot(left_high, right_high, preferred_element_type=F32)


def residual_kernel(where_ref, first_ref, second_ref, live_ref, tables_ref,
                    measured_ref, low_ref, high_ref, waves, backs):
    strip_rows, group, window = first_ref.shape
    share = group // 2
    rows = strip_rows * share

    def by_columns(high, low, table):
        return three_products(high, low, tables_ref[table], tables_ref[table + 1])

    for half in range(2):
        block = (first_ref if half == 0 else second_ref)[...]
        wide = jnp.concatenate(
            [block[:, :share].reshape(rows, window), block[:, share:].reshape(rows, window)], axis=1
        )
        high, low = split_two(wide)
        done = by_columns(high, low, 0)
        for c in range(2):
            waves[c, half * rows : (half + 1) * rows, :] = done[:, c * window : (c + 1) * window]

    for p in range(0, share, 2):
        columns = []
        for k in range(2):
            columns.append(
                jnp.concatenate(
                    [waves[c, pl.ds(p + k, window, stride=share), :] for c in range(2)], axis=0
                )
            )
        high, low = split_two(jnp.concatenate(columns, axis=1))
        far = three_products(tables_ref[4], tables_ref[5], high, low)
        far_re, far_im = far[:window], far[window:]
        measured = jnp.concatenate([measured_ref[p], measured_ref[p + 1]], axis=1)
        modulus = jnp.sqrt(far_re * far_re + far_im * far_im + ETA)
        keep_share = 1.0 - measured / modulus
        high, low = split_two(jnp.concatenate([far_re * keep_share, far_im * keep_share], axis=0))
        back = three_products(tables_ref[6], tables_ref[7], high, low)
        for k in range(2):
            for c in range(2):
                backs[c, pl.ds(p + k, window, stride=share), :] = back[
                    c * window : (c + 1) * window, k * window : (k + 1) * window
                ]

    for half, out_ref in ((0, low_ref), (1, high_ref)):
        wide = jnp.concatenate(
            [backs[c, half * rows : (half + 1) * rows, :] for c in range(2)], axis=1
        )
        high, low = split_two(wide)
        done = by_columns(high, low, 2)
        for c in range(2):
            piece = done[:, c * window : (c + 1) * window].reshape(strip_rows, share, window)
            piece = piece * live_ref[...][None]
            out_ref[:, c * share : (c + 1) * share, :] = piece.astype(BF16)


def residual(where, first, second, live, tables, amplitude):
    strip_rows, group, window = first.shape
    share = group // 2
    whole = pl.BlockSpec(first.shape, lambda i, w: (0, 0, 0))
    return pl.pallas_call(
        residual_kernel,
        grid_spec=pltpu.PrefetchScalarGridSpec(
            num_scalar_prefetch=1,
            grid=(1,),
            in_specs=[
                whole,
                whole,
                pl.BlockSpec(live.shape, lambda i, w: (0, 0)),
                pl.BlockSpec(tables.shape, lambda i, w: (0, 0, 0)),
                pl.BlockSpec((share, window, window), lambda i, w: (w[0], 0, 0)),
            ],
            out_specs=[whole, whole],
            scratch_shapes=[
                pltpu.VMEM((2, window * share, window), F32),
                pltpu.VMEM((2, window * share, window), F32),
            ],
        ),
        out_shape=[jax.ShapeDtypeStruct(first.shape, BF16)] * 2,
        compiler_params=pltpu.CompilerParams(vmem_limit_bytes=48 << 20),
        cost_estimate=pl.CostEstimate(
            flops=24 * share * 4 * window**3 * 2,
            bytes_accessed=16 * first.size,
            transcendentals=0,
        ),
    )(where, first, second, live, tables, amplitude)


def transform_tables(window):
    counter = np.arange(window)
    turn_angle = (counter[:, None] * counter[None, :] % window) * (2.0 * np.pi / window)
    table_re = np.cos(turn_angle) / np.sqrt(window)
    table_im = -np.sin(turn_angle) / np.sqrt(window)
    stacked = []
    for left in (False, True):
        for sign in (1.0, -1.0):
            imag = sign * table_im
            if left:
                full = np.block([[table_re, -imag], [imag, table_re]])
            else:
                full = np.block([[table_re, imag], [-imag, table_re]])
            high = full.astype(BF16)
            stacked += [high, (full - high.astype(np.float64)).astype(BF16)]
    return jnp.asarray(np.stack(stacked))


def share_order(shares):
    order = [0]
    bit = shares // 2
    while bit:
        order = order + [o | bit for o in order]
        bit //= 2
    return order


def body(smatrix, beam_freq, beam_amp, row_offset, col_offset, counts, amplitude):
    beam_dev = smatrix.shape[1]
    strip_rows = smatrix.shape[2]
    window = smatrix.shape[3]
    per_tile = row_offset.shape[0]
    scan_size = lax.axis_size("scan")
    shares = lax.axis_size("beam")
    share_rows = per_tile // shares
    field_rows = strip_rows * scan_size
    assert window == 2 * strip_rows
    my_tile = lax.axis_index("scan")
    my_beam = lax.axis_index("beam")
    order = share_order(shares)

    offsets = jnp.stack([row_offset, col_offset])
    offset_sets = [offsets] + [passed_along(offsets, "scan", d) for d in (1, 2)]
    stacked = jnp.stack(offset_sets).reshape(3, 2, shares, share_rows)
    stacked = jnp.take(stacked, jnp.array(order, jnp.int32) ^ my_beam, axis=2)
    rows = stacked[:, 0]
    cols = stacked[:, 1]
    distance = jnp.arange(3, dtype=jnp.int32)[:, None, None]
    tile_ids = (my_tile - distance) % scan_size
    coef_re, coef_im = coefficients(
        (tile_ids * strip_rows + rows).reshape(-1),
        cols.reshape(-1),
        beam_freq,
        beam_amp,
        field_rows,
        window,
    )
    real_rows = jnp.concatenate([coef_re, -coef_im], axis=1)
    imag_rows = jnp.concatenate([coef_im, coef_re], axis=1)
    matrix = jnp.stack(
        [
            real_rows.reshape(3 * shares, share_rows, 2 * beam_dev),
            imag_rows.reshape(3 * shares, share_rows, 2 * beam_dev),
        ],
        axis=1,
    ).reshape(6 * per_tile, 2 * beam_dev)
    low = jnp.where(distance == 0, rows, 0)
    high = jnp.where(distance == 2, rows, strip_rows)
    bounds = jnp.stack([low, high])[:, :, :, None, :]
    bounds = jnp.broadcast_to(bounds, (2, 3, shares, 2, share_rows)).reshape(2, 6 * per_tile, 1)
    bounds = jnp.broadcast_to(bounds, (2, 6 * per_tile, window))
    first_row = my_beam * share_rows
    live = (first_row + jnp.arange(share_rows, dtype=jnp.int32) < counts[0]).astype(F32)
    live = jnp.broadcast_to(live[:, None], (share_rows, window))
    tables = transform_tables(window)

    near, far = forward(matrix, bounds, smatrix, shares, scan_size)
    near, far = residual(my_beam.reshape(1), near, far, live, tables, amplitude)
    strips = [near, passed_along(far, "scan", 1), passed_along(near, "scan", 2)]
    parts = []
    for strip in strips:
        held = [strip]
        bit = shares // 2
        while bit:
            held = held + [swapped(h, "beam", bit) for h in held]
            bit //= 2
        parts += held
    return backward(matrix.T, bounds, parts, shares, beam_dev)


def solution(mesh):
    return jax.shard_map(
        body,
        mesh=mesh,
        in_specs=(
            P(None, "beam", "scan", None),
            P(None, "beam"),
            P(None, "beam"),
            P("scan"),
            P("scan"),
            P("scan"),
            P("scan", None, None),
        ),
        out_specs=P(None, "beam", "scan", None),
        check_vma=False,
    )
```
